32 devices in a mesh: parts: 2 (over y), row: 4 (over x, core), col: 4 (over z).
Axes of the slice: x: 2, y: 2, z: 4, core: 2. Of those that a mesh axis runs over, the one named last changes fastest.
Arguments:
- left_factor: bfloat16 [6144, 8, 1024], P(('parts', 'col'), None, 'row'), parts along dimension 0, may hold values from -0.109375 to 0.109375
- right_factor: bfloat16 [64, 1024, 3072], P('parts', 'col', 'row'), parts along dimension 0, may hold values from -6 to 6
- amplitudes: bfloat16 [1024, 1024, 512], P('row', 'col', 'parts'), parts along dimension 2, may hold values from -0.0078125 to 0.0078125
Outputs:
- ladder: float32 [512, 256], P(('parts', 'row', 'col')), parts along dimension 0
The draws below stay inside these ranges and needn't reach their ends.
There are 2 independent parts, one for each index of `parts`. The reference program is written for one: setup_inputs(seed, part) draws one part's arguments, and reference() takes and returns one part's arrays. A program takes and returns all parts, laid end to end along the dimension named above; each array names one. Nothing has to cross between parts.
All inputs are finite; a program needn't handle non-finite values.
Results may differ from the reference program's by a relative error of at most 0.0029.
Values may be sent and summed in bfloat16 or wider, within the bound.
A program may use at most 192 MiB of HBM per device.

```python
import jax
import jax.numpy as jnp
from jax import lax

V = 1024
NAUX = 3072
NA = 8
NB = 32
P_SIZE = 256


def strengthened(array, key, source, target, parts, factor):
    def block_of(position):
        return (jnp.arange(array.shape[position]) // (array.shape[position] // parts)).reshape((-1,) + (1,) * (array.ndim - 1 - position))

    near = jax.random.permutation(key, parts)[block_of(target)]
    second = (block_of(target) + parts // 2) % parts
    return jnp.where((block_of(source) == near) | (block_of(source) == second), factor * array, array)


def shard_levels(key, dims, cuts, low, top_value):
    gain = 1.0
    for axis_at, shards_of in cuts:
        steps = jax.random.uniform(jax.random.fold_in(jax.random.fold_in(key, 6), axis_at), (shards_of,), jnp.float32, low / len(cuts), top_value / len(cuts))
        gain = gain * jnp.repeat(jnp.exp(steps), dims[axis_at] // shards_of).reshape((-1,) + (1,) * (len(dims) - 1 - axis_at))
    return gain


def gaussian(key, shape, scale, most, pieces=(), dtype=jnp.bfloat16):
    array = jax.random.normal(key, shape, jnp.float32) * scale
    if len(pieces) > 0:
        array = shard_levels(key, shape, pieces, -0.22, 0.18) * array
    return jnp.clip(array, min=-most, max=most).astype(dtype)


def heavy_noise(rng, extent, spread, most, shards, heavy, dtype=jnp.bfloat16):
    values = spread * jax.random.normal(rng, extent, jnp.float32)
    if shards:
        values = values * shard_levels(rng, extent, shards, -0.22, 0.18)
    return jnp.clip(strengthened(values, jax.random.fold_in(rng, 3), *heavy), -most, most).astype(dtype)


def setup_inputs(seed: int = 0, part: int = 0) -> dict:
    seeds = jax.random.split(jax.random.key(seed), 4)
    own_keys = jax.random.split(jax.random.fold_in(seeds[3], part), 4)
    return {
        "left_factor": gaussian(own_keys[0], (NAUX, NA, V), NAUX ** -0.5, 0.109375, ((0, 4), (2, 4))),
        "right_factor": gaussian(own_keys[1], (NB, V, NAUX), 1.0, 6.0, ((1, 4), (2, 4))),
        "amplitudes": heavy_noise(own_keys[2], (V, V, P_SIZE), (V * V) ** -0.5, 0.0078125, ((0, 4), (1, 4)), (1, 2, 4, 2.0)),
    }


def reference(left_factor, right_factor, amplitudes):
    right_flat = right_factor.reshape(NB * V, NAUX)
    amp_flat = amplitudes.reshape(V * V, P_SIZE)

    def one_virtual(left_slice):
        integral = lax.dot_general(left_slice, right_flat, (((0,), (1,)), ((), ())), preferred_element_type=jnp.float32).astype(jnp.bfloat16)
        ordered = integral.reshape(V, NB, V).transpose(0, 2, 1).reshape(V * V, NB)
        return lax.dot_general(amp_flat, ordered, (((0,), (0,)), ((), ())), preferred_element_type=jnp.float32)

    stacked = lax.map(one_virtual, jnp.moveaxis(left_factor, 1, 0))
    return jnp.transpose(stacked, (1, 0, 2)).reshape(P_SIZE, NA * NB)
```

```python
import functools

import jax
import jax.numpy as jnp
from jax import lax
from jax.experimental import pallas as pl
from jax.experimental.pallas import tpu as pltpu
from jax.sharding import PartitionSpec as P

MESH = pl.DeviceIdType.MESH
HALVES = 2
GROUP = 8
C_STEP = 8
ROW_TILE = 512


def ladder_kernel(
    n_row, n_col, left_ref, right_ref, amp_ref, out_ref, others_ref,
    left_all, right_buf, integral, amp_buf, total, total_t, row_in, row_sum, col_in,
    own_sem, load_sem, amp_sem, l_send, l_recv, x_send, x_recv, s_send, s_recv, f_send, f_recv,
    r1_send, r1_recv, r2_send, r2_recv,
):
    rows_all, aux = left_ref.shape
    width_b, span_d, _ = right_ref.shape
    span_c, _, pairs = amp_ref.shape
    width_a = rows_all // span_c
    part_rows = rows_all // HALVES
    groups = width_b // GROUP
    r = lax.axis_index("row")
    k = lax.axis_index("col")
    mate = r + 1 - 2 * lax.rem(r, 2)
    across = lax.rem(r + 2, 4)
    diagonal = 3 - r

    barrier = pltpu.get_barrier_semaphore()
    for step in range(1, n_row):
        pl.semaphore_signal(barrier, inc=1, device_id={"row": lax.rem(r + step, n_row)}, device_id_type=MESH)
    for step in range(1, n_col):
        pl.semaphore_signal(barrier, inc=1, device_id={"col": lax.rem(k + step, n_col)}, device_id_type=MESH)
    pl.semaphore_wait(barrier, n_row + n_col - 2)

    def columns(q):
        return pl.ds(pl.multiple_of(q * aux, 128), aux)

    def left_copy(part, source, way, own):
        rows = pl.ds(part * part_rows, part_rows)
        place = left_all.at[rows, columns(source)]
        return pltpu.make_async_remote_copy(
            src_ref=left_ref.at[rows] if own else place,
            dst_ref=place,
            send_sem=l_send.at[part, source, way],
            recv_sem=l_recv.at[part, source],
            device_id={"col": k + 1 - 2 * way},
            device_id_type=MESH,
        )

    def left_own(part, act):
        @pl.when(k + 1 < n_col)
        def _():
            act(left_copy(part, k, 0, True))

        @pl.when(k >= 1)
        def _():
            act(left_copy(part, k, 1, True))

    def left_step(part, step):
        @pl.when(k >= step)
        def _():
            left_copy(part, k - step, 0, False).wait_recv()

            @pl.when(k + 1 < n_col)
            def _():
                left_copy(part, k - step, 0, False).start()

        @pl.when(k + step < n_col)
        def _():
            left_copy(part, k + step, 1, False).wait_recv()

            @pl.when(k >= 1)
            def _():
                left_copy(part, k + step, 1, False).start()

    def left_drain(part, step):
        @pl.when((k >= step) & (k + 1 < n_col))
        def _():
            left_copy(part, k - step, 0, False).wait_send()

        @pl.when((k + step < n_col) & (k >= 1))
        def _():
            left_copy(part, k + step, 1, False).wait_send()

    def mate_copy(b):
        return pltpu.make_async_remote_copy(
            src_ref=right_ref.at[b], dst_ref=others_ref.at[0, b], send_sem=s_send.at[b],
            recv_sem=s_recv.at[b], device_id={"row": mate}, device_id_type=MESH)

    def across_copy(b):
        return pltpu.make_async_remote_copy(
            src_ref=right_ref.at[b], dst_ref=others_ref.at[1, b], send_sem=x_send.at[b],
            recv_sem=x_recv.at[b], device_id={"row": across}, device_id_type=MESH)

    def onward_copy(b):
        return pltpu.make_async_remote_copy(
            src_ref=others_ref.at[1, b], dst_ref=others_ref.at[2, b], send_sem=f_send.at[b],
            recv_sem=f_recv.at[b], device_id={"row": mate}, device_id_type=MESH)

    def forward(b):
        across_copy(b).wait_recv()
        onward_copy(b).start()

    def settle(b):
        mate_copy(b).wait_recv()
        onward_copy(b).wait_recv()

    def loads(b, slot):
        sources = ((right_ref.at[b], r), (others_ref.at[0, b], mate), (others_ref.at[1, b], across), (others_ref.at[2, b], diagonal))
        return [
            pltpu.make_async_copy(source, right_buf.at[slot, :, columns(q)], load_sem.at[slot, x])
            for x, (source, q) in enumerate(sources)
        ]

    def load_start(b, slot):
        for copy in loads(b, slot):
            copy.start()

    def load_wait(b, slot):
        for copy in loads(b, slot):
            copy.wait()

    def amp_copy(c, slot):
        return pltpu.make_async_copy(amp_ref.at[pl.ds(c, C_STEP)], amp_buf.at[slot], amp_sem.at[slot])

    def contract(bi, slot, first_row, row_count):
        def tile(n, _):
            at = pl.multiple_of(n * ROW_TILE, ROW_TILE)
            integral[bi, pl.ds(at, ROW_TILE), :] = lax.dot_general(
                left_all[pl.ds(pl.multiple_of(first_row + at, ROW_TILE), ROW_TILE), :], right_buf[slot],
                (((1,), (1,)), ((), ())), preferred_element_type=jnp.float32)
            return 0

        lax.fori_loop(0, row_count // ROW_TILE, tile, 0)

    def unit(part, parts, group, first, forward_from=None, forward_count=0, done=0):
        first_row = part * part_rows
        row_count = parts * part_rows
        c_start = first_row // width_a
        blocks = row_count // width_a // C_STEP
        amp_copy(c_start, 0).start()
        base = group * GROUP
        if first:
            def body(bi, _):
                b = base + bi
                slot = lax.rem(bi, 2)

                @pl.when(bi >= done)
                def _():
                    forward(b)

                settle(b)
                load_start(b, slot)
                load_wait(b, slot)
                contract(bi, slot, first_row, row_count)
                return 0
        else:
            load_start(base, 0)

            def body(bi, _):
                slot = lax.rem(bi, 2)
                load_wait(base + bi, slot)

                @pl.when(bi + 1 < GROUP)
                def _():
                    load_start(base + bi + 1, 1 - slot)

                if forward_count:
                    every = GROUP // forward_count

                    @pl.when(lax.rem(bi, every) == every - 1)
                    def _():
                        forward(forward_from + bi // every)

                contract(bi, slot, first_row, row_count)
                return 0

        lax.fori_loop(0, GROUP, body, 0)
        group_rows = pl.ds(group * GROUP * width_a, GROUP * width_a)

        def close(n, _):
            slot = lax.rem(n, 2)
            amp_copy(c_start + n * C_STEP, slot).wait()

            @pl.when(n + 1 < blocks)
            def _():
                amp_copy(c_start + (n + 1) * C_STEP, 1 - slot).start()

            pieces = []
            for c in range(C_STEP):
                at = pl.multiple_of((n * C_STEP + c) * width_a, 8)
                piece = integral[:, pl.ds(at, width_a), :]
                pieces.append(piece.reshape(GROUP * width_a, span_d).astype(jnp.bfloat16))
            total[group_rows, :] += jnp.dot(
                jnp.concatenate(pieces, axis=1), amp_buf[slot].reshape(C_STEP * span_d, pairs),
                preferred_element_type=jnp.float32)
            return 0

        lax.fori_loop(0, blocks, close, 0)

    own_copy = pltpu.make_async_copy(left_ref, left_all.at[:, columns(k)], own_sem)
    left_own(0, lambda copy: copy.start())

    def send_right(b, _):
        across_copy(b).start()
        mate_copy(b).start()
        return 0

    lax.fori_loop(0, width_b, send_right, 0)
    own_copy.start()
    total[...] = jnp.zeros_like(total)

    steps = n_col - 1
    for step in range(1, steps + 1):
        if step == steps:
            left_own(1, lambda copy: copy.start())
        left_step(0, step)
    own_copy.wait()

    lead = groups - 1
    marks = {}
    for step in range(1, steps + 1):
        marks.setdefault(min(step, lead), []).append(step)
    for group in range(lead):
        for step in marks.get(group, []):
            left_step(1, step)
        unit(0, 1, group, True)
    for step in marks.get(lead, []):
        left_step(1, step)
    per_unit = 2
    for group in range(lead):
        unit(1, 1, group, False, lead * GROUP + group * per_unit, per_unit)
    unit(0, 2, lead, True, done=lead * per_unit)

    total_t[...] = total[...].T
    block1 = pairs // n_row

    def row_copy(q):
        return pltpu.make_async_remote_copy(
            src_ref=total_t.at[pl.ds(pl.multiple_of(q * block1, 8), block1)], dst_ref=row_in.at[r],
            send_sem=r1_send.at[q], recv_sem=r1_recv.at[r], device_id={"row": q}, device_id_type=MESH)

    def row_arrival(q):
        return pltpu.make_async_remote_copy(
            src_ref=total_t.at[pl.ds(0, block1)], dst_ref=row_in.at[q],
            send_sem=r1_send.at[q], recv_sem=r1_recv.at[q], device_id={"row": q}, device_id_type=MESH)

    for step in range(1, n_row):
        row_copy(lax.rem(r + step, n_row)).start()
    value = total_t[pl.ds(pl.multiple_of(r * block1, 8), block1), :]
    for step in range(1, n_row):
        q = lax.rem(r + step, n_row)
        row_arrival(q).wait_recv()
        value += row_in[q]
    row_sum[...] = value
    block2 = block1 // n_col

    def col_copy(q):
        return pltpu.make_async_remote_copy(
            src_ref=row_sum.at[pl.ds(pl.multiple_of(q * block2, 8), block2)], dst_ref=col_in.at[k],
            send_sem=r2_send.at[q], recv_sem=r2_recv.at[k], device_id={"col": q}, device_id_type=MESH)

    def col_arrival(q):
        return pltpu.make_async_remote_copy(
            src_ref=row_sum.at[pl.ds(0, block2)], dst_ref=col_in.at[q],
            send_sem=r2_send.at[q], recv_sem=r2_recv.at[q], device_id={"col": q}, device_id_type=MESH)

    for step in range(1, n_col):
        col_copy(lax.rem(k + step, n_col)).start()
    result = row_sum[pl.ds(pl.multiple_of(k * block2, 8), block2), :]
    for step in range(1, n_col):
        q = lax.rem(k + step, n_col)
        col_arrival(q).wait_recv()
        result += col_in[q]
    out_ref[...] = result

    for step in range(1, n_row):
        row_copy(lax.rem(r + step, n_row)).wait_send()
    for step in range(1, n_col):
        col_copy(lax.rem(k + step, n_col)).wait_send()
    for part in range(HALVES):
        left_own(part, lambda copy: copy.wait_send())
        for step in range(1, steps + 1):
            left_drain(part, step)

    def drain(b, _):
        across_copy(b).wait_send()
        mate_copy(b).wait_send()
        onward_copy(b).wait_send()
        return 0

    lax.fori_loop(0, width_b, drain, 0)


def fused(n_row, n_col, left_factor, right_factor, amplitudes):
    aux, width_a, span_c = left_factor.shape
    width_b, span_d, _ = right_factor.shape
    pairs = amplitudes.shape[2]
    rows = width_a * span_c
    left_rows = jnp.transpose(left_factor, (2, 1, 0)).reshape(rows, aux)
    anywhere = pl.BlockSpec(memory_space=pl.ANY)
    dma = pltpu.SemaphoreType.DMA
    block1 = pairs // n_row
    summed, _ = pl.pallas_call(
        functools.partial(ladder_kernel, n_row, n_col),
        out_shape=(
            jax.ShapeDtypeStruct((block1 // n_col, width_a * width_b), jnp.float32),
            jax.ShapeDtypeStruct((n_row - 1,) + right_factor.shape, jnp.bfloat16),
        ),
        in_specs=[anywhere] * 3,
        out_specs=(pl.BlockSpec(memory_space=pltpu.VMEM), anywhere),
        scratch_shapes=[
            pltpu.VMEM((rows, aux * n_col), jnp.bfloat16),
            pltpu.VMEM((2, span_d, aux * n_row), jnp.bfloat16),
            pltpu.VMEM((GROUP, rows, span_d), jnp.float32),
            pltpu.VMEM((2, C_STEP, span_d, pairs), jnp.bfloat16),
            pltpu.VMEM((width_a * width_b, pairs), jnp.float32),
            pltpu.VMEM((pairs, width_a * width_b), jnp.float32),
            pltpu.VMEM((n_row, block1, width_a * width_b), jnp.float32),
            pltpu.VMEM((block1, width_a * width_b), jnp.float32),
            pltpu.VMEM((n_col, block1 // n_col, width_a * width_b), jnp.float32),
            dma, dma((2, 4)), dma((2,)),
            dma((HALVES, n_col, 2)), dma((HALVES, n_col)),
            dma((width_b,)), dma((width_b,)), dma((width_b,)), dma((width_b,)), dma((width_b,)), dma((width_b,)),
            dma((n_row,)), dma((n_row,)), dma((n_col,)), dma((n_col,)),
        ],
        compiler_params=pltpu.CompilerParams(
            collective_id=0, has_side_effects=True, vmem_limit_bytes=60 * 1024 * 1024),
    )(left_rows, right_factor, amplitudes)
    pair_count = summed.shape[0]
    return jnp.transpose(summed.reshape(pair_count, width_b, width_a), (0, 2, 1)).reshape(pair_count, width_a * width_b)


def plain(left_factor, right_factor, amplitudes):
    aux, width_a, span_c = left_factor.shape
    width_b, span_d, _ = right_factor.shape
    left_all = lax.all_gather(left_factor, "col", axis=0, tiled=True)
    left_flat = left_all.reshape(left_all.shape[0], width_a * span_c)
    right_all = lax.all_gather(right_factor, "row", axis=2, tiled=True)
    integral = lax.dot_general(
        left_flat, right_all.reshape(width_b * span_d, right_all.shape[2]),
        (((0,), (1,)), ((), ())), preferred_element_type=jnp.float32)
    rounded = integral.astype(jnp.bfloat16).reshape(width_a, span_c, width_b, span_d)
    partial_sums = jnp.einsum(
        "cdp,acbd->pab", amplitudes, rounded, preferred_element_type=jnp.float32
    ).reshape(amplitudes.shape[2], width_a * width_b)
    return lax.psum_scatter(partial_sums, ("row", "col"), scatter_dimension=0, tiled=True)


def on_device(n_row, n_col, left_factor, right_factor, amplitudes):
    aux, width_a, span_c = left_factor.shape
    width_b, span_d, right_aux = right_factor.shape
    pairs = amplitudes.shape[2]
    fits = (
        n_row == 4 and n_col == 4 and aux == right_aux and aux % 128 == 0 and width_a % 8 == 0
        and span_d % 128 == 0 and width_b == 4 * GROUP and pairs % (8 * n_row * n_col) == 0
        and (width_a * span_c) % (HALVES * ROW_TILE) == 0 and span_c % (HALVES * C_STEP) == 0
    )
    if fits:
        return fused(n_row, n_col, left_factor, right_factor, amplitudes)
    return plain(left_factor, right_factor, amplitudes)


def solution(mesh):
    return jax.shard_map(
        functools.partial(on_device, mesh.shape["row"], mesh.shape["col"]),
        mesh=mesh,
        in_specs=(
            P(("parts", "col"), None, "row"),
            P("parts", "col", "row"),
            P("row", "col", "parts"),
        ),
        out_specs=P(("parts", "row", "col"), None),
        check_vma=False,
    )
```

```python
import functools

import jax
import jax.numpy as jnp
from jax import lax
from jax.experimental import pallas as pl
from jax.experimental.pallas import tpu as pltpu
from jax.sharding import PartitionSpec as P

MESH = pl.DeviceIdType.MESH
HALVES = 2
GROUP = 8
C_STEP = 8
ROW_TILE = 1024


def ladder_kernel(
    n_row, n_col, left_ref, right_ref, amp_ref, out_ref, others_ref,
    left_all, right_buf, integral, amp_buf, total, total_t, row_in, row_sum, col_in,
    own_sem, load_sem, amp_sem, l_send, l_recv, x_send, x_recv, s_send, s_recv, f_send, f_recv,
    r1_send, r1_recv, r2_send, r2_recv,
):
    rows_all, aux = left_ref.shape
    width_b, span_d, _ = right_ref.shape
    span_c, _, pairs = amp_ref.shape
    width_a = rows_all // span_c
    part_rows = rows_all // HALVES
    groups = width_b // GROUP
    r = lax.axis_index("row")
    k = lax.axis_index("col")
    mate = r + 1 - 2 * lax.rem(r, 2)
    across = lax.rem(r + 2, 4)
    diagonal = 3 - r

    barrier = pltpu.get_barrier_semaphore()
    for step in range(1, n_row):
        pl.semaphore_signal(barrier, inc=1, device_id={"row": lax.rem(r + step, n_row)}, device_id_type=MESH)
    for step in range(1, n_col):
        pl.semaphore_signal(barrier, inc=1, device_id={"col": lax.rem(k + step, n_col)}, device_id_type=MESH)
    pl.semaphore_wait(barrier, n_row + n_col - 2)

    def columns(q):
        return pl.ds(pl.multiple_of(q * aux, 128), aux)

    def left_copy(part, source, way, own):
        rows = pl.ds(part * part_rows, part_rows)
        place = left_all.at[rows, columns(source)]
        return pltpu.make_async_remote_copy(
            src_ref=left_ref.at[rows] if own else place,
            dst_ref=place,
            send_sem=l_send.at[part, source, way],
            recv_sem=l_recv.at[part, source],
            device_id={"col": k + 1 - 2 * way},
            device_id_type=MESH,
        )

    def left_own(part, act):
        @pl.when(k + 1 < n_col)
        def _():
            act(left_copy(part, k, 0, True))

        @pl.when(k >= 1)
        def _():
            act(left_copy(part, k, 1, True))

    def left_step(part, step):
        @pl.when(k >= step)
        def _():
            left_copy(part, k - step, 0, False).wait_recv()

            @pl.when(k + 1 < n_col)
            def _():
                left_copy(part, k - step, 0, False).start()

        @pl.when(k + step < n_col)
        def _():
            left_copy(part, k + step, 1, False).wait_recv()

            @pl.when(k >= 1)
            def _():
                left_copy(part, k + step, 1, False).start()

    def left_drain(part, step):
        @pl.when((k >= step) & (k + 1 < n_col))
        def _():
            left_copy(part, k - step, 0, False).wait_send()

        @pl.when((k + step < n_col) & (k >= 1))
        def _():
            left_copy(part, k + step, 1, False).wait_send()

    def mate_copy(b):
        return pltpu.make_async_remote_copy(
            src_ref=right_ref.at[b], dst_ref=others_ref.at[0, b], send_sem=s_send.at[b],
            recv_sem=s_recv.at[b], device_id={"row": mate}, device_id_type=MESH)

    def across_copy(b):
        return pltpu.make_async_remote_copy(
            src_ref=right_ref.at[b], dst_ref=others_ref.at[1, b], send_sem=x_send.at[b],
            recv_sem=x_recv.at[b], device_id={"row": across}, device_id_type=MESH)

    def onward_copy(b):
        return pltpu.make_async_remote_copy(
            src_ref=others_ref.at[1, b], dst_ref=others_ref.at[2, b], send_sem=f_send.at[b],
            recv_sem=f_recv.at[b], device_id={"row": mate}, device_id_type=MESH)

    def forward(b):
        across_copy(b).wait_recv()
        onward_copy(b).start()

    def settle(b):
        mate_copy(b).wait_recv()
        onward_copy(b).wait_recv()

    def loads(b, slot):
        sources = ((right_ref.at[b], r), (others_ref.at[0, b], mate), (others_ref.at[1, b], across), (others_ref.at[2, b], diagonal))
        return [
            pltpu.make_async_copy(source, right_buf.at[slot, :, columns(q)], load_sem.at[slot, x])
            for x, (source, q) in enumerate(sources)
        ]

    def load_start(b, slot):
        for copy in loads(b, slot):
            copy.start()

    def load_wait(b, slot):
        for copy in loads(b, slot):
            copy.wait()

    def amp_copy(c, slot):
        return pltpu.make_async_copy(amp_ref.at[pl.ds(c, C_STEP)], amp_buf.at[slot], amp_sem.at[slot])

    def contract(bi, slot, first_row, row_count):
        def tile(n, _):
            at = pl.multiple_of(n * ROW_TILE, ROW_TILE)
            integral[bi, pl.ds(at, ROW_TILE), :] = lax.dot_general(
                left_all[pl.ds(pl.multiple_of(first_row + at, ROW_TILE), ROW_TILE), :], right_buf[slot],
                (((1,), (1,)), ((), ())), preferred_element_type=jnp.float32)
            return 0

        lax.fori_loop(0, row_count // ROW_TILE, tile, 0)

    def unit(part, parts, group, first, forward_from=None, forward_count=0, done=0):
        first_row = part * part_rows
        row_count = parts * part_rows
        c_start = first_row // width_a
        blocks = row_count // width_a // C_STEP
        amp_copy(c_start, 0).start()
        base = group * GROUP
        if first:
            def body(bi, _):
                b = base + bi
                slot = lax.rem(bi, 2)

                @pl.when(bi >= done)
                def _():
                    forward(b)

                settle(b)
                load_start(b, slot)
                load_wait(b, slot)
                contract(bi, slot, first_row, row_count)
                return 0
        else:
            load_start(base, 0)

            def body(bi, _):
                slot = lax.rem(bi, 2)
                load_wait(base + bi, slot)

                @pl.when(bi + 1 < GROUP)
                def _():
                    load_start(base + bi + 1, 1 - slot)

                if forward_count:
                    every = GROUP // forward_count

                    @pl.when(lax.rem(bi, every) == every - 1)
                    def _():
                        forward(forward_from + bi // every)

                contract(bi, slot, first_row, row_count)
                return 0

        lax.fori_loop(0, GROUP, body, 0)
        group_rows = pl.ds(group * GROUP * width_a, GROUP * width_a)

        def close(n, _):
            slot = lax.rem(n, 2)
            amp_copy(c_start + n * C_STEP, slot).wait()

            @pl.when(n + 1 < blocks)
            def _():
                amp_copy(c_start + (n + 1) * C_STEP, 1 - slot).start()

            pieces = []
            for c in range(C_STEP):
                at = pl.multiple_of((n * C_STEP + c) * width_a, 8)
                piece = integral[:, pl.ds(at, width_a), :]
                pieces.append(piece.reshape(GROUP * width_a, span_d).astype(jnp.bfloat16))
            total[group_rows, :] += jnp.dot(
                jnp.concatenate(pieces, axis=1), amp_buf[slot].reshape(C_STEP * span_d, pairs),
                preferred_element_type=jnp.float32)
            return 0

        lax.fori_loop(0, blocks, close, 0)

    own_copy = pltpu.make_async_copy(left_ref, left_all.at[:, columns(k)], own_sem)
    left_own(0, lambda copy: copy.start())

    def send_right(b, _):
        across_copy(b).start()
        mate_copy(b).start()
        return 0

    lax.fori_loop(0, width_b, send_right, 0)
    own_copy.start()
    total[...] = jnp.zeros_like(total)

    steps = n_col - 1
    for step in range(1, steps + 1):
        if step == steps:
            left_own(1, lambda copy: copy.start())
        left_step(0, step)
    own_copy.wait()

    lead = groups - 1
    marks = {}
    for step in range(1, steps + 1):
        marks.setdefault(min(step, lead), []).append(step)
    for group in range(lead):
        for step in marks.get(group, []):
            left_step(1, step)
        unit(0, 1, group, True)
    for step in marks.get(lead, []):
        left_step(1, step)
    per_unit = 2
    for group in range(lead):
        unit(1, 1, group, False, lead * GROUP + group * per_unit, per_unit)
    unit(0, 2, lead, True, done=lead * per_unit)

    total_t[...] = total[...].T
    block1 = pairs // n_row

    def row_copy(q):
        return pltpu.make_async_remote_copy(
            src_ref=total_t.at[pl.ds(pl.multiple_of(q * block1, 8), block1)], dst_ref=row_in.at[r],
            send_sem=r1_send.at[q], recv_sem=r1_recv.at[r], device_id={"row": q}, device_id_type=MESH)

    def row_arrival(q):
        return pltpu.make_async_remote_copy(
            src_ref=total_t.at[pl.ds(0, block1)], dst_ref=row_in.at[q],
            send_sem=r1_send.at[q], recv_sem=r1_recv.at[q], device_id={"row": q}, device_id_type=MESH)

    for step in range(1, n_row):
        row_copy(lax.rem(r + step, n_row)).start()
    value = total_t[pl.ds(pl.multiple_of(r * block1, 8), block1), :]
    for step in range(1, n_row):
        q = lax.rem(r + step, n_row)
        row_arrival(q).wait_recv()
        value += row_in[q]
    row_sum[...] = value
    block2 = block1 // n_col

    def col_copy(q):
        return pltpu.make_async_remote_copy(
            src_ref=row_sum.at[pl.ds(pl.multiple_of(q * block2, 8), block2)], dst_ref=col_in.at[k],
            send_sem=r2_send.at[q], recv_sem=r2_recv.at[k], device_id={"col": q}, device_id_type=MESH)

    def col_arrival(q):
        return pltpu.make_async_remote_copy(
            src_ref=row_sum.at[pl.ds(0, block2)], dst_ref=col_in.at[q],
            send_sem=r2_send.at[q], recv_sem=r2_recv.at[q], device_id={"col": q}, device_id_type=MESH)

    for step in range(1, n_col):
        col_copy(lax.rem(k + step, n_col)).start()
    result = row_sum[pl.ds(pl.multiple_of(k * block2, 8), block2), :]
    for step in range(1, n_col):
        q = lax.rem(k + step, n_col)
        col_arrival(q).wait_recv()
        result += col_in[q]
    out_ref[...] = result

    for step in range(1, n_row):
        row_copy(lax.rem(r + step, n_row)).wait_send()
    for step in range(1, n_col):
        col_copy(lax.rem(k + step, n_col)).wait_send()
    for part in range(HALVES):
        left_own(part, lambda copy: copy.wait_send())
        for step in range(1, steps + 1):
            left_drain(part, step)

    def drain(b, _):
        across_copy(b).wait_send()
        mate_copy(b).wait_send()
        onward_copy(b).wait_send()
        return 0

    lax.fori_loop(0, width_b, drain, 0)


def fused(n_row, n_col, left_factor, right_factor, amplitudes):
    aux, width_a, span_c = left_factor.shape
    width_b, span_d, _ = right_factor.shape
    pairs = amplitudes.shape[2]
    rows = width_a * span_c
    left_rows = jnp.transpose(left_factor, (2, 1, 0)).reshape(rows, aux)
    anywhere = pl.BlockSpec(memory_space=pl.ANY)
    dma = pltpu.SemaphoreType.DMA
    block1 = pairs // n_row
    summed, _ = pl.pallas_call(
        functools.partial(ladder_kernel, n_row, n_col),
        out_shape=(
            jax.ShapeDtypeStruct((block1 // n_col, width_a * width_b), jnp.float32),
            jax.ShapeDtypeStruct((n_row - 1,) + right_factor.shape, jnp.bfloat16),
        ),
        in_specs=[anywhere] * 3,
        out_specs=(pl.BlockSpec(memory_space=pltpu.VMEM), anywhere),
        scratch_shapes=[
            pltpu.VMEM((rows, aux * n_col), jnp.bfloat16),
            pltpu.VMEM((2, span_d, aux * n_row), jnp.bfloat16),
            pltpu.VMEM((GROUP, rows, span_d), jnp.float32),
            pltpu.VMEM((2, C_STEP, span_d, pairs), jnp.bfloat16),
            pltpu.VMEM((width_a * width_b, pairs), jnp.float32),
            pltpu.VMEM((pairs, width_a * width_b), jnp.float32),
            pltpu.VMEM((n_row, block1, width_a * width_b), jnp.float32),
            pltpu.VMEM((block1, width_a * width_b), jnp.float32),
            pltpu.VMEM((n_col, block1 // n_col, width_a * width_b), jnp.float32),
            dma, dma((2, 4)), dma((2,)),
            dma((HALVES, n_col, 2)), dma((HALVES, n_col)),
            dma((width_b,)), dma((width_b,)), dma((width_b,)), dma((width_b,)), dma((width_b,)), dma((width_b,)),
            dma((n_row,)), dma((n_row,)), dma((n_col,)), dma((n_col,)),
        ],
        compiler_params=pltpu.CompilerParams(
            collective_id=0, has_side_effects=True, vmem_limit_bytes=60 * 1024 * 1024),
    )(left_rows, right_factor, amplitudes)
    pair_count = summed.shape[0]
    return jnp.transpose(summed.reshape(pair_count, width_b, width_a), (0, 2, 1)).reshape(pair_count, width_a * width_b)


def plain(left_factor, right_factor, amplitudes):
    aux, width_a, span_c = left_factor.shape
    width_b, span_d, _ = right_factor.shape
    left_all = lax.all_gather(left_factor, "col", axis=0, tiled=True)
    left_flat = left_all.reshape(left_all.shape[0], width_a * span_c)
    right_all = lax.all_gather(right_factor, "row", axis=2, tiled=True)
    integral = lax.dot_general(
        left_flat, right_all.reshape(width_b * span_d, right_all.shape[2]),
        (((0,), (1,)), ((), ())), preferred_element_type=jnp.float32)
    rounded = integral.astype(jnp.bfloat16).reshape(width_a, span_c, width_b, span_d)
    partial_sums = jnp.einsum(
        "cdp,acbd->pab", amplitudes, rounded, preferred_element_type=jnp.float32
    ).reshape(amplitudes.shape[2], width_a * width_b)
    return lax.psum_scatter(partial_sums, ("row", "col"), scatter_dimension=0, tiled=True)


def on_device(n_row, n_col, left_factor, right_factor, amplitudes):
    aux, width_a, span_c = left_factor.shape
    width_b, span_d, right_aux = right_factor.shape
    pairs = amplitudes.shape[2]
    fits = (
        n_row == 4 and n_col == 4 and aux == right_aux and aux % 128 == 0 and width_a % 8 == 0
        and span_d % 128 == 0 and width_b == 4 * GROUP and pairs % (8 * n_row * n_col) == 0
        and (width_a * span_c) % (HALVES * ROW_TILE) == 0 and span_c % (HALVES * C_STEP) == 0
    )
    if fits:
        return fused(n_row, n_col, left_factor, right_factor, amplitudes)
    return plain(left_factor, right_factor, amplitudes)


def solution(mesh):
    return jax.shard_map(
        functools.partial(on_device, mesh.shape["row"], mesh.shape["col"]),
        mesh=mesh,
        in_specs=(
            P(("parts", "col"), None, "row"),
            P("parts", "col", "row"),
            P("row", "col", "parts"),
        ),
        out_specs=P(("parts", "row", "col"), None),
        check_vma=False,
    )
```
